32 devices in a mesh: depth: 8 (over y, x, core), row: 4 (over z).
Axes of the slice: x: 2, y: 2, z: 4, core: 2. Of those that a mesh axis runs over, the one named last changes fastest.
Arguments:
- input_cells: bfloat16 [32, 64, 128, 128], P('depth', 'row'), may hold values from -6 to 6
- first_weight: bfloat16 [3, 3, 3, 64, 128], P(None, None, None, None, 'depth'), may hold values from -0.15625 to 0.15625
- second_weight: bfloat16 [3, 3, 3, 128, 256], P(None, None, None, None, 'depth'), may hold values from -0.109375 to 0.109375
Outputs:
- encoded: bfloat16 [8, 16, 32, 512], P('depth', 'row')
The draws below stay inside these ranges and needn't reach their ends.
All inputs are finite; a program needn't handle non-finite values.
Results may differ from the reference program's by a relative error of at most 0.0049.
Values may be sent and summed in bfloat16 or wider, within the bound.
A program may use at most 64 MiB of HBM per device.

```python
import math
import jax
import jax.numpy as jnp
from jax import lax

IN_CH = 64
MID_CH = 128
OUT_CH = 256
CELLS_W = 256
DEPTH = 32
ROWS = 64


def block_scale(rng, dims, split, smallest, largest):
    loudness, own = 1.0, jax.random.fold_in(rng, 6)
    for dim, shards_of in split:
        heights = jnp.exp(jax.random.uniform(jax.random.fold_in(own, dim), (shards_of,), jnp.float32, smallest / len(split), largest / len(split)))
        loudness = loudness * jnp.repeat(heights, dims[dim] // shards_of).reshape([-1 if axis == dim else 1 for axis in range(len(dims))])
    return loudness


def centred(stream_key, shape, deviation, bound, pieces=(), kind=jnp.bfloat16):
    result = jax.random.normal(stream_key, shape, jnp.float32) * deviation
    if len(pieces) > 0:
        result = block_scale(stream_key, shape, pieces, -0.22, 0.18) * result
    return jnp.clip(result, min=-bound, max=bound).astype(kind)


def setup_inputs(seed: int = 0) -> dict:
    key_of = jax.random.split(jax.random.key(seed), 4)
    return {
        "input_cells": centred(key_of[0], (DEPTH, ROWS, CELLS_W // 2, 2 * IN_CH), 1.0, 6.0, ((0, 8), (1, 4))),
        "first_weight": centred(key_of[1], (3, 3, 3, IN_CH, MID_CH), (27 * IN_CH) ** -0.5, 0.15625, ((4, 8),)),
        "second_weight": centred(key_of[2], (3, 3, 3, MID_CH, OUT_CH), (27 * MID_CH) ** -0.5, 0.109375, ((4, 8),)),
    }


def stacked(weight, depth_tap, row_tap):
    kernel_taps = weight[depth_tap, row_tap]
    zeros_block = jnp.zeros_like(kernel_taps[0])
    upper_part = jnp.concatenate([kernel_taps[1], kernel_taps[2]], 0)
    lower_part = jnp.concatenate([zeros_block, kernel_taps[0]], 0)
    return jnp.concatenate([upper_part, lower_part], 1)


def convolve(extended, weight):
    planes = extended.shape[0] - 1
    row_count = extended.shape[1] - 1
    pair_count = extended.shape[2]
    features = extended.shape[3]
    out_width = weight.shape[4]
    running = jnp.zeros(((planes // 2) * (row_count // 2) * pair_count, 2 * out_width), jnp.float32)
    for depth_tap in range(3):
        for row_tap in range(3):
            window = extended[depth_tap:depth_tap + planes:2, row_tap:row_tap + row_count:2]
            running = running + jnp.dot(window.reshape(-1, features), stacked(weight, depth_tap, row_tap), preferred_element_type=jnp.float32)
    running = running.reshape(planes // 2, row_count // 2, pair_count, 2 * out_width)
    carried = jnp.pad(running[:, :, :-1, out_width:], ((0, 0), (0, 0), (1, 0), (0, 0)))
    return running[..., :out_width] + carried


def finish(field):
    activated = jnp.maximum(field, 0.0).astype(jnp.bfloat16)
    shape_now = activated.shape
    return activated.reshape(shape_now[0], shape_now[1], shape_now[2] // 2, 2 * shape_now[3])


def layer(field, weight):
    extended = jnp.pad(field, ((1, 0), (1, 0), (0, 0), (0, 0)))
    planes = field.shape[0]
    block = math.gcd(planes // 2, 8)
    block_count = planes // 2 // block

    def one_block(block_index):
        slab_cells = lax.dynamic_slice_in_dim(extended, (block_index * 2 * block).astype(jnp.int32), 2 * block + 1, 0)
        return finish(convolve(slab_cells, weight))

    blocks = lax.map(one_block, jnp.arange(block_count, dtype=jnp.int32))
    return blocks.reshape((planes // 2,) + blocks.shape[2:])


def reference(input_cells, first_weight, second_weight):
    hidden = layer(input_cells, first_weight)
    return layer(hidden, second_weight)
```

```python
import functools

import jax
import jax.numpy as jnp
from jax import lax
from jax.experimental import pallas as pl
from jax.experimental.pallas import tpu as pltpu
from jax.sharding import PartitionSpec as P

MESH = pl.DeviceIdType.MESH
BF16, F32 = jnp.bfloat16, jnp.float32


def dot_nt(lhs, rhs):
    return lax.dot_general(lhs, rhs, (((1,), (1,)), ((), ())), preferred_element_type=F32)


def merged(block):
    n, ch, k = block.shape
    if ch % 16 == 0:
        return block.reshape(n * ch, k)
    return jnp.concatenate([block[s].astype(F32) for s in range(n)], 0).astype(BF16)


def shift_pairs(low, pairs):
    rolled = pltpu.roll(low, 1, 0)
    at = lax.broadcasted_iota(jnp.int32, low.shape, 0)
    return jnp.where(lax.rem(at, pairs) == 0, 0.0, rolled)


def kernel(n, rows_n, x_ref, w1_ref, w2_ref, o_ref, ext, g1, g2, hid, tmp, tmp2,
           x_sem, own_sem, h_send, h_recv, w1_send, w1_fwd, w1_recv,
           w2_send, w2_fwd, w2_recv, hh_send, hh_recv):
    d, r = lax.axis_index("depth"), lax.axis_index("row")
    planes, qs = x_ref.shape[0], x_ref.shape[1]
    pairs, feats = x_ref.shape[3], x_ref.shape[4]
    c1 = feats // 2
    mid = n * w1_ref.shape[1]
    out_ch = n * w2_ref.shape[1]
    hplanes, hrows = planes // 2, qs
    hq = hrows // 2
    hpairs = pairs // 2

    has_next_d, has_prev_d = d < n - 1, d > 0
    has_next_r, has_prev_r = r < rows_n - 1, r > 0
    parity = lax.rem(d, 2)
    partner = d + 1 - 2 * parity

    own_x = [
        pltpu.make_async_copy(x_ref.at[:, :, 0], ext.at[1:planes + 1, 0:qs, 1], x_sem.at[0]),
        pltpu.make_async_copy(x_ref.at[:, :, 1], ext.at[1:planes + 1, 1:qs + 1, 0], x_sem.at[1]),
    ]
    for c in own_x:
        c.start()
    own_w2 = pltpu.make_async_copy(w2_ref, g2.at[:, d], own_sem.at[0])
    own_w2.start()

    barrier = pltpu.get_barrier_semaphore()
    for k in range(1, n):
        pl.semaphore_signal(barrier, inc=1, device_id=(lax.rem(d + k, n), r), device_id_type=MESH)

    @pl.when(has_next_r)
    def _():
        pl.semaphore_signal(barrier, inc=1, device_id=(d, r + 1), device_id_type=MESH)

    @pl.when(has_prev_r)
    def _():
        pl.semaphore_signal(barrier, inc=1, device_id=(d, r - 1), device_id_type=MESH)

    @pl.when(has_next_r & has_next_d)
    def _():
        pl.semaphore_signal(barrier, inc=1, device_id=(d + 1, r + 1), device_id_type=MESH)

    @pl.when(has_prev_r & has_prev_d)
    def _():
        pl.semaphore_signal(barrier, inc=1, device_id=(d - 1, r - 1), device_id_type=MESH)

    zero_half = jnp.zeros((w1_ref.shape[1], c1), BF16)
    for ij in range(9):
        g1[ij, d] = jnp.concatenate([w1_ref[3 * ij + 1], w1_ref[3 * ij + 2]], 1)
        g1[9 + ij, d] = jnp.concatenate([zero_half, w1_ref[3 * ij]], 1)

    @pl.when(jnp.logical_not(has_prev_d))
    def _():
        ext[0] = jnp.zeros(ext.shape[1:], BF16)
        hid[0] = jnp.zeros(hid.shape[1:], BF16)

    @pl.when(jnp.logical_not(has_prev_r))
    def _():
        ext[:, 0, 0] = jnp.zeros((planes + 1, pairs, feats), BF16)
        hid[:, 0, 0] = jnp.zeros((hplanes + 1, hpairs, 2 * mid), BF16)

    expected = (n - 1 + has_next_r.astype(jnp.int32) + has_prev_r.astype(jnp.int32)
                + (has_next_r & has_next_d).astype(jnp.int32)
                + (has_prev_r & has_prev_d).astype(jnp.int32))
    pl.semaphore_wait(barrier, expected)

    def remote(src, dst, ssem, rsem, to):
        return pltpu.make_async_remote_copy(
            src_ref=src, dst_ref=dst, send_sem=ssem, recv_sem=rsem,
            device_id=to, device_id_type=MESH)

    def weight_copy(src, buf, owner, ssem, rsem, to):
        return remote(src, buf.at[:, owner], ssem, rsem.at[owner], (to, r))

    def same(k):
        return lax.rem(d + 2 * k, n)

    w1_out = [weight_copy(g1.at[:, d], g1, d, w1_send.at[0], w1_recv, partner)]
    w2_out = [weight_copy(w2_ref, g2, d, w2_send.at[0], w2_recv, partner)]
    for k in range(1, n // 2):
        w1_out.append(weight_copy(g1.at[:, d], g1, d, w1_send.at[k], w1_recv, same(k)))
        w2_out.append(weight_copy(w2_ref, g2, d, w2_send.at[k], w2_recv, same(k)))
    w1_on = [weight_copy(g1.at[:, same(k)], g1, same(k), w1_fwd.at[k], w1_recv, partner) for k in range(1, n // 2)]
    w2_on = [weight_copy(g2.at[:, same(k)], g2, same(k), w2_fwd.at[k], w2_recv, partner) for k in range(1, n // 2)]

    def arrived(buf, rsem, owner):
        remote(buf.at[:, owner], buf.at[:, owner], rsem.at[owner], rsem.at[owner], (partner, r)).wait_recv()

    next_d, next_r = lax.rem(d + 1, n), lax.rem(r + 1, rows_n)
    plane_out = [
        remote(x_ref.at[planes - 1, :, 0], ext.at[0, 0:qs, 1], h_send.at[0], h_recv.at[0], (next_d, r)),
        remote(x_ref.at[planes - 1, :, 1], ext.at[0, 1:qs + 1, 0], h_send.at[1], h_recv.at[1], (next_d, r)),
    ]
    row_out = [remote(x_ref.at[:, qs - 1, 1], ext.at[1:planes + 1, 0, 0], h_send.at[2], h_recv.at[2], (d, next_r))]
    corner_out = [remote(x_ref.at[planes - 1, qs - 1, 1], ext.at[0, 0, 0], h_send.at[3], h_recv.at[3], (next_d, next_r))]

    def when_start(cond, copies):
        @pl.when(cond)
        def _():
            for c in copies:
                c.start()

    def when_recv(cond, copies):
        @pl.when(cond)
        def _():
            for c in copies:
                c.wait_recv()

    def when_sent(cond, copies):
        @pl.when(cond)
        def _():
            for c in copies:
                c.wait_send()

    for c in w1_out:
        c.start()
    when_start(has_next_r, row_out)
    when_start(has_next_d, plane_out)
    when_start(has_next_d & has_next_r, corner_out)
    for c in w2_out:
        c.start()

    for k in range(1, n // 2):
        arrived(g1, w1_recv, same(k))
        w1_on[k - 1].start()
    for k in range(0, n // 2):
        arrived(g1, w1_recv, lax.rem(partner + 2 * k, n))
    for c in own_x:
        c.wait()
    when_recv(has_prev_r, row_out)

    rhs1 = jnp.concatenate(
        [jnp.concatenate([merged(g1[ij]), merged(g1[9 + ij])], 0) for ij in range(9)], 1)

    def first(a):
        wins = []
        for i in range(3):
            for j in range(3):
                w = ext[2 * a + i, j // 2:j // 2 + qs, j % 2]
                wins.append(w.reshape(qs * pairs, feats))
        res = dot_nt(jnp.concatenate(wins, 1), rhs1)
        val = jnp.maximum(res[:, :mid] + shift_pairs(res[:, mid:], pairs), 0.0)
        tmp[...] = val
        half = qs * hpairs
        for s in range(2):
            part = tmp[pl.ds(s, half, 2), :].astype(BF16).reshape(hq, 2, hpairs, mid)
            hid[a + 1, 0:hq, 1, :, s * mid:(s + 1) * mid] = part[:, 0]
            hid[a + 1, 1:hq + 1, 0, :, s * mid:(s + 1) * mid] = part[:, 1]

    last = hplanes
    hplane_out = [
        remote(hid.at[last, 0:hq, 1], hid.at[0, 0:hq, 1], hh_send.at[0], hh_recv.at[0], (next_d, r)),
        remote(hid.at[last, 1:hq + 1, 0], hid.at[0, 1:hq + 1, 0], hh_send.at[1], hh_recv.at[1], (next_d, r)),
    ]
    hcorner_out = [remote(hid.at[last, hq, 0], hid.at[0, 0, 0], hh_send.at[2], hh_recv.at[2], (next_d, next_r))]
    hrow_out = [remote(hid.at[a + 1, hq, 0], hid.at[a + 1, 0, 0], hh_send.at[3 + a], hh_recv.at[3 + a], (d, next_r))
                for a in range(hplanes)]

    for a in range(hplanes - 1, -1, -1):
        if a == 0:
            when_recv(has_prev_d, plane_out)
            when_recv(has_prev_d & has_prev_r, corner_out)
        first(a)
        if a == hplanes - 1:
            when_start(has_next_d, hplane_out)
            when_start(has_next_d & has_next_r, hcorner_out)
        when_start(has_next_r, [hrow_out[a]])

    for k in range(1, n // 2):
        arrived(g2, w2_recv, same(k))
        w2_on[k - 1].start()
    for k in range(0, n // 2):
        arrived(g2, w2_recv, lax.rem(partner + 2 * k, n))
    own_w2.wait()
    when_recv(has_prev_r, hrow_out)
    when_recv(has_prev_d, hplane_out)
    when_recv(has_prev_d & has_prev_r, hcorner_out)

    for a in range(hplanes // 2):
        wins, rights, ups, lows = [], [], [], []
        for i in range(3):
            for j in range(3):
                w = hid[2 * a + i, j // 2:j // 2 + hq, j % 2].reshape(hq * hpairs, 2 * mid)
                wins.append(w)
                rights.append(w[:, mid:])
                t = 3 * (3 * i + j)
                ups += [merged(g2[t + 1]), merged(g2[t + 2])]
                lows.append(merged(g2[t]))
        up = dot_nt(jnp.concatenate(wins, 1), jnp.concatenate(ups, 1))
        low = dot_nt(jnp.concatenate(rights, 1), jnp.concatenate(lows, 1))
        val = jnp.maximum(up + shift_pairs(low, hpairs), 0.0)
        half = hq * hpairs // 2
        for h in range(out_ch // 128):
            tmp2[h] = val[:, h * 128:(h + 1) * 128]
        for s in range(2):
            for h in range(out_ch // 128):
                part = tmp2[h, pl.ds(s, half, 2), :].astype(BF16).reshape(hq, hpairs // 2, 128)
                at = s * out_ch + h * 128
                o_ref[a, :, :, at:at + 128] = part

    for c in w1_out + w1_on + w2_out + w2_on:
        c.wait_send()
    when_sent(has_next_r, row_out + hrow_out)
    when_sent(has_next_d, plane_out + hplane_out)
    when_sent(has_next_d & has_next_r, corner_out + hcorner_out)


def solution(mesh):
    n, rows_n = mesh.shape["depth"], mesh.shape["row"]

    def per_device(x, w1, w2):
        planes, rows, pairs, feats = x.shape
        ch1, ch2 = w1.shape[4], w2.shape[4]
        mid, out_ch = n * ch1, n * ch2
        qs = rows // 2
        hplanes, hq, hpairs = planes // 2, rows // 4, pairs // 2
        x5 = x.reshape(planes, qs, 2, pairs, feats)
        w1t = jnp.transpose(w1, (0, 1, 2, 4, 3)).reshape(27, ch1, w1.shape[3])
        w2t = jnp.transpose(w2, (0, 1, 2, 4, 3)).reshape(27, ch2, w2.shape[3])
        dma = pltpu.SemaphoreType.DMA
        return pl.pallas_call(
            functools.partial(kernel, n, rows_n),
            out_shape=jax.ShapeDtypeStruct((planes // 4, rows // 4, pairs // 4, 2 * out_ch), BF16),
            in_specs=[pl.BlockSpec(memory_space=pl.ANY), pl.BlockSpec(memory_space=pltpu.VMEM),
                      pl.BlockSpec(memory_space=pl.ANY)],
            out_specs=pl.BlockSpec(memory_space=pltpu.VMEM),
            scratch_shapes=[
                pltpu.VMEM((planes + 1, qs + 1, 2, pairs, feats), BF16),
                pltpu.VMEM((18, n, ch1, feats), BF16),
                pltpu.VMEM((27, n, ch2, mid), BF16),
                pltpu.VMEM((hplanes + 1, hq + 1, 2, hpairs, 2 * mid), BF16),
                pltpu.VMEM((qs * pairs, mid), F32),
                pltpu.VMEM((out_ch // 128, hq * hpairs, 128), F32),
                dma((2,)), dma((1,)), dma((4,)), dma((4,)),
                dma((n // 2,)), dma((n // 2,)), dma((n,)),
                dma((n // 2,)), dma((n // 2,)), dma((n,)),
                dma((3 + hplanes,)), dma((3 + hplanes,)),
            ],
            compiler_params=pltpu.CompilerParams(
                collective_id=0, has_side_effects=True, vmem_limit_bytes=60 * 1024 * 1024),
        )(x5, w1t, w2t)

    return jax.shard_map(
        per_device,
        mesh=mesh,
        in_specs=(
            P("depth", "row", None, None),
            P(None, None, None, None, "depth"),
            P(None, None, None, None, "depth"),
        ),
        out_specs=P("depth", "row", None, None),
        check_vma=False,
    )
```

```python
import functools

import jax
import jax.numpy as jnp
from jax import lax
from jax.experimental import pallas as pl
from jax.experimental.pallas import tpu as pltpu
from jax.sharding import PartitionSpec as P

MESH = pl.DeviceIdType.MESH
BF16, F32 = jnp.bfloat16, jnp.float32
CUTS1 = (0, 18)
CUTS2 = (0, 9, 18, 27)


def dot_nt(lhs, rhs):
    return lax.dot_general(lhs, rhs, (((1,), (1,)), ((), ())), preferred_element_type=F32)


def merged(block):
    n, ch, k = block.shape
    if ch % 16 == 0:
        return block.reshape(n * ch, k)
    return jnp.concatenate([block[s].astype(F32) for s in range(n)], 0).astype(BF16)


def shift_pairs(low, pairs):
    rolled = pltpu.roll(low, 1, 0)
    at = lax.broadcasted_iota(jnp.int32, low.shape, 0)
    return jnp.where(lax.rem(at, pairs) == 0, 0.0, rolled)


def kernel(n, rows_n, x_ref, w1_ref, w2_ref, o_ref, ext, g1, g2, hid, tmp, tmp2,
           x_sem, own_sem, h_send, h_recv, w1_send, w1_recv,
           w2_send, w2_recv, hh_send, hh_recv):
    d, r = lax.axis_index("depth"), lax.axis_index("row")
    planes, qs = x_ref.shape[0], x_ref.shape[1]
    pairs, feats = x_ref.shape[3], x_ref.shape[4]
    c1 = feats // 2
    mid = n * w1_ref.shape[1]
    out_ch = n * w2_ref.shape[1]
    hplanes, hrows = planes // 2, qs
    hq = hrows // 2
    hpairs = pairs // 2

    has_next_d, has_prev_d = d < n - 1, d > 0
    has_next_r, has_prev_r = r < rows_n - 1, r > 0
    parity = lax.rem(d, 2)
    partner = d + 1 - 2 * parity

    own_x = [
        pltpu.make_async_copy(x_ref.at[:, :, 0], ext.at[1:planes + 1, 0:qs, 1], x_sem.at[0]),
        pltpu.make_async_copy(x_ref.at[:, :, 1], ext.at[1:planes + 1, 1:qs + 1, 0], x_sem.at[1]),
    ]
    for c in own_x:
        c.start()
    own_w2 = pltpu.make_async_copy(w2_ref, g2.at[:, d], own_sem.at[0])
    own_w2.start()

    barrier = pltpu.get_barrier_semaphore()
    relay = n == 8 and rows_n % 2 == 0
    if relay:
        chip, core = d // 2, lax.rem(d, 2)
        x_nbr = chip + 1 - 2 * lax.rem(chip, 2)
        y_nbr = chip + 2 - 4 * (chip // 2)
        mate_r = r + 1 - 2 * lax.rem(r, 2)
        turned = chip == 2
        u_nbr = jnp.where(turned, x_nbr, y_nbr)
        v_nbr = jnp.where(turned, y_nbr, x_nbr)
        g_nbr = 3 - chip
        mine = core == lax.rem(r, 2)
        friends = [(partner, r), (2 * x_nbr + core, r), (2 * y_nbr + core, r), (d, mate_r)]
    else:
        friends = [(lax.rem(d + k, n), r) for k in range(1, n)]
    for to in friends:
        pl.semaphore_signal(barrier, inc=1, device_id=to, device_id_type=MESH)

    @pl.when(has_prev_d)
    def _():
        pl.semaphore_signal(barrier, inc=1, device_id=(d - 1, r), device_id_type=MESH)

    @pl.when(has_prev_r)
    def _():
        pl.semaphore_signal(barrier, inc=1, device_id=(d, r - 1), device_id_type=MESH)

    @pl.when(has_prev_r & has_prev_d)
    def _():
        pl.semaphore_signal(barrier, inc=1, device_id=(d - 1, r - 1), device_id_type=MESH)

    zero_half = jnp.zeros((w1_ref.shape[1], c1), BF16)
    for ij in range(9):
        g1[ij, d] = jnp.concatenate([w1_ref[3 * ij + 1], w1_ref[3 * ij + 2]], 1)
        g1[9 + ij, d] = jnp.concatenate([zero_half, w1_ref[3 * ij]], 1)

    @pl.when(jnp.logical_not(has_prev_d))
    def _():
        ext[0] = jnp.zeros(ext.shape[1:], BF16)
        hid[0] = jnp.zeros(hid.shape[1:], BF16)

    @pl.when(jnp.logical_not(has_prev_r))
    def _():
        ext[:, 0, 0] = jnp.zeros((planes + 1, pairs, feats), BF16)
        hid[:, 0, 0] = jnp.zeros((hplanes + 1, hpairs, 2 * mid), BF16)

    expected = (len(friends) + has_next_d.astype(jnp.int32) + has_next_r.astype(jnp.int32)
                + (has_next_r & has_next_d).astype(jnp.int32))
    pl.semaphore_wait(barrier, expected)

    def remote(src, dst, ssem, rsem, to):
        return pltpu.make_async_remote_copy(
            src_ref=src, dst_ref=dst, send_sem=ssem, recv_sem=rsem,
            device_id=to, device_id_type=MESH)

    def when_start(cond, copies):
        @pl.when(cond)
        def _():
            for c in copies:
                c.start()

    def when_recv(cond, copies):
        @pl.when(cond)
        def _():
            for c in copies:
                c.wait_recv()

    def when_sent(cond, copies):
        @pl.when(cond)
        def _():
            for c in copies:
                c.wait_send()

    always = n > 0
    sent = []

    class Gather:
        def __init__(self, buf, own, ssem, rsem, cuts):
            self.buf, self.own, self.ssem, self.rsem = buf, own, ssem, rsem
            self.cuts = list(zip(cuts[:-1], cuts[1:]))
            self.used = 0

        def copy(self, owner, j, to, own=False):
            lo, hi = self.cuts[j]
            place = self.buf.at[lo:hi, owner]
            c = remote(self.own.at[lo:hi] if own else place, place, self.ssem.at[self.used],
                       self.rsem.at[owner * len(self.cuts) + j], to)
            self.used += 1
            return c

        def send(self, cond, owner, j, to, own=False):
            c = self.copy(owner, j, to, own)
            sent.append((cond, c))
            if cond is always:
                c.start()
            else:
                when_start(cond, [c])

        def wait(self, owner, j):
            lo, hi = self.cuts[j]
            place = self.buf.at[lo:hi, owner]
            sem = self.rsem.at[owner * len(self.cuts) + j]
            remote(place, place, sem, sem, (partner, r)).wait_recv()

        def send_own(self):
            for j in range(len(self.cuts)):
                if relay:
                    self.send((chip == 3) | mine, d, j, (2 * x_nbr + core, r), True)
                    self.send((chip != 0) | mine, d, j, (2 * y_nbr + core, r), True)
                else:
                    for k in range(1, n // 2):
                        self.send(always, d, j, (lax.rem(d + 2 * k, n), r), True)
            for j in range(len(self.cuts)):
                self.send(always, d, j, (partner, r), True)

        def stage(self, which, j):
            if not relay:
                if which == "g":
                    for k in range(1, n // 2):
                        self.wait(lax.rem(d + 2 * k, n), j)
                        self.send(always, lax.rem(d + 2 * k, n), j, (partner, r))
                return
            owner = 2 * {"u": u_nbr, "v": v_nbr, "g": g_nbr}[which] + core
            self.wait(owner, j)
            if which == "u":
                self.send(mine & (chip >= 2), owner, j, (2 * jnp.where(turned, y_nbr, x_nbr) + core, r))
            if which == "v":
                self.send(mine & ((chip == 1) | (chip == 3)), owner, j, (2 * y_nbr + core, r))
            if which != "u":
                self.send(mine, owner, j, (d, mate_r))
            self.send(always, owner, j, (partner, r))

        def rest(self):
            for j in range(len(self.cuts)):
                for k in range(0, n // 2):
                    self.wait(lax.rem(partner + 2 * k, n), j)

    gather1 = Gather(g1, g1.at[:, d], w1_send, w1_recv, CUTS1)
    gather2 = Gather(g2, w2_ref, w2_send, w2_recv, CUTS2)

    next_d, next_r = lax.rem(d + 1, n), lax.rem(r + 1, rows_n)
    plane_out = [
        remote(x_ref.at[planes - 1, :, 0], ext.at[0, 0:qs, 1], h_send.at[0], h_recv.at[0], (next_d, r)),
        remote(x_ref.at[planes - 1, :, 1], ext.at[0, 1:qs + 1, 0], h_send.at[1], h_recv.at[1], (next_d, r)),
    ]
    row_out = [remote(x_ref.at[:, qs - 1, 1], ext.at[1:planes + 1, 0, 0], h_send.at[2], h_recv.at[2], (d, next_r))]
    corner_out = [remote(x_ref.at[planes - 1, qs - 1, 1], ext.at[0, 0, 0], h_send.at[3], h_recv.at[3], (next_d, next_r))]

    gather1.send_own()
    when_start(has_next_r, row_out)
    gather2.send_own()
    when_start(has_next_d, plane_out)
    when_start(has_next_d & has_next_r, corner_out)

    for which in "uvg":
        for j in range(len(CUTS1) - 1):
            gather1.stage(which, j)
    gather1.rest()
    for c in own_x:
        c.wait()
    when_recv(has_prev_r, row_out)

    rhs1 = jnp.concatenate(
        [jnp.concatenate([merged(g1[ij]), merged(g1[9 + ij])], 0) for ij in range(9)], 1)

    def first(a):
        wins = []
        for i in range(3):
            for j in range(3):
                w = ext[2 * a + i, j // 2:j // 2 + qs, j % 2]
                wins.append(w.reshape(qs * pairs, feats))
        res = dot_nt(jnp.concatenate(wins, 1), rhs1)
        val = jnp.maximum(res[:, :mid] + shift_pairs(res[:, mid:], pairs), 0.0)
        tmp[...] = val
        half = qs * hpairs
        for s in range(2):
            part = tmp[pl.ds(s, half, 2), :].astype(BF16).reshape(hq, 2, hpairs, mid)
            hid[a + 1, 0:hq, 1, :, s * mid:(s + 1) * mid] = part[:, 0]
            hid[a + 1, 1:hq + 1, 0, :, s * mid:(s + 1) * mid] = part[:, 1]

    last = hplanes
    hplane_out = [
        remote(hid.at[last, 0:hq, 1], hid.at[0, 0:hq, 1], hh_send.at[0], hh_recv.at[0], (next_d, r)),
        remote(hid.at[last, 1:hq + 1, 0], hid.at[0, 1:hq + 1, 0], hh_send.at[1], hh_recv.at[1], (next_d, r)),
    ]
    hcorner_out = [remote(hid.at[last, hq, 0], hid.at[0, 0, 0], hh_send.at[2], hh_recv.at[2], (next_d, next_r))]
    hrow_out = [remote(hid.at[a + 1, hq, 0], hid.at[a + 1, 0, 0], hh_send.at[3 + a], hh_recv.at[3 + a], (d, next_r))
                for a in range(hplanes)]

    for a in range(hplanes - 1, -1, -1):
        if a == 0:
            when_recv(has_prev_d, plane_out)
            when_recv(has_prev_d & has_prev_r, corner_out)
        first(a)
        if a == hplanes - 1:
            when_start(has_next_d, hplane_out)
            when_start(has_next_d & has_next_r, hcorner_out)
        when_start(has_next_r, [hrow_out[a]])
        if a == hplanes - 1:
            for which in "uv":
                for j in range(len(CUTS2) - 1):
                    gather2.stage(which, j)

    for j in range(len(CUTS2) - 1):
        gather2.stage("g", j)
    gather2.rest()
    own_w2.wait()
    when_recv(has_prev_r, hrow_out)
    when_recv(has_prev_d, hplane_out)
    when_recv(has_prev_d & has_prev_r, hcorner_out)

    for a in range(hplanes // 2):
        wins, rights, ups, lows = [], [], [], []
        for i in range(3):
            for j in range(3):
                w = hid[2 * a + i, j // 2:j // 2 + hq, j % 2].reshape(hq * hpairs, 2 * mid)
                wins.append(w)
                rights.append(w[:, mid:])
                t = 3 * (3 * i + j)
                ups += [merged(g2[t + 1]), merged(g2[t + 2])]
                lows.append(merged(g2[t]))
        up = dot_nt(jnp.concatenate(wins, 1), jnp.concatenate(ups, 1))
        low = dot_nt(jnp.concatenate(rights, 1), jnp.concatenate(lows, 1))
        val = jnp.maximum(up + shift_pairs(low, hpairs), 0.0)
        half = hq * hpairs // 2
        for h in range(out_ch // 128):
            tmp2[h] = val[:, h * 128:(h + 1) * 128]
        for s in range(2):
            for h in range(out_ch // 128):
                part = tmp2[h, pl.ds(s, half, 2), :].astype(BF16).reshape(hq, hpairs // 2, 128)
                at = s * out_ch + h * 128
                o_ref[a, :, :, at:at + 128] = part

    for cond, c in sent:
        when_sent(cond, [c])
    when_sent(has_next_r, row_out + hrow_out)
    when_sent(has_next_d, plane_out + hplane_out)
    when_sent(has_next_d & has_next_r, corner_out + hcorner_out)


def solution(mesh):
    n, rows_n = mesh.shape["depth"], mesh.shape["row"]

    def per_device(x, w1, w2):
        planes, rows, pairs, feats = x.shape
        ch1, ch2 = w1.shape[4], w2.shape[4]
        mid, out_ch = n * ch1, n * ch2
        qs = rows // 2
        hplanes, hq, hpairs = planes // 2, rows // 4, pairs // 2
        x5 = x.reshape(planes, qs, 2, pairs, feats)
        w1t = jnp.transpose(w1, (0, 1, 2, 4, 3)).reshape(27, ch1, w1.shape[3])
        w2t = jnp.transpose(w2, (0, 1, 2, 4, 3)).reshape(27, ch2, w2.shape[3])
        dma = pltpu.SemaphoreType.DMA
        sends = max(n, 11)
        return pl.pallas_call(
            functools.partial(kernel, n, rows_n),
            out_shape=jax.ShapeDtypeStruct((planes // 4, rows // 4, pairs // 4, 2 * out_ch), BF16),
            in_specs=[pl.BlockSpec(memory_space=pl.ANY), pl.BlockSpec(memory_space=pltpu.VMEM),
                      pl.BlockSpec(memory_space=pl.ANY)],
            out_specs=pl.BlockSpec(memory_space=pltpu.VMEM),
            scratch_shapes=[
                pltpu.VMEM((planes + 1, qs + 1, 2, pairs, feats), BF16),
                pltpu.VMEM((18, n, ch1, feats), BF16),
                pltpu.VMEM((27, n, ch2, mid), BF16),
                pltpu.VMEM((hplanes + 1, hq + 1, 2, hpairs, 2 * mid), BF16),
                pltpu.VMEM((qs * pairs, mid), F32),
                pltpu.VMEM((out_ch // 128, hq * hpairs, 128), F32),
                dma((2,)), dma((1,)), dma((4,)), dma((4,)),
                dma((sends * (len(CUTS1) - 1),)), dma((n * (len(CUTS1) - 1),)),
                dma((sends * (len(CUTS2) - 1),)), dma((n * (len(CUTS2) - 1),)),
                dma((3 + hplanes,)), dma((3 + hplanes,)),
            ],
            compiler_params=pltpu.CompilerParams(
                collective_id=0, has_side_effects=True, vmem_limit_bytes=60 * 1024 * 1024),
        )(x5, w1t, w2t)

    return jax.shard_map(
        per_device,
        mesh=mesh,
        in_specs=(
            P("depth", "row", None, None),
            P(None, None, None, None, "depth"),
            P(None, None, None, None, "depth"),
        ),
        out_specs=P("depth", "row", None, None),
        check_vma=False,
    )
```

```python
import functools

import jax
import jax.numpy as jnp
from jax import lax
from jax.experimental import pallas as pl
from jax.experimental.pallas import tpu as pltpu
from jax.sharding import PartitionSpec as P

MESH = pl.DeviceIdType.MESH
BF16, F32 = jnp.bfloat16, jnp.float32
CUTS1 = (0, 18)
CUTS2 = (0, 9, 18, 27)


def dot_nt(lhs, rhs):
    return lax.dot_general(lhs, rhs, (((1,), (1,)), ((), ())), preferred_element_type=F32)


def merged(block):
    n, ch, k = block.shape
    if ch % 16 == 0:
        return block.reshape(n * ch, k)
    return jnp.concatenate([block[s].astype(F32) for s in range(n)], 0).astype(BF16)


def shift_pairs(low, pairs):
    rolled = pltpu.roll(low, 1, 0)
    at = lax.broadcasted_iota(jnp.int32, low.shape, 0)
    return jnp.where(lax.rem(at, pairs) == 0, 0.0, rolled)


def kernel(n, rows_n, x_ref, w1_ref, w2_ref, o_ref, ext, g1, g2, hid, tmp, tmp2,
           x_sem, own_sem, h_send, h_recv, w1_send, w1_recv,
           w2_send, w2_recv, hh_send, hh_recv):
    d, r = lax.axis_index("depth"), lax.axis_index("row")
    planes, qs = x_ref.shape[0], x_ref.shape[1]
    pairs, feats = x_ref.shape[3], x_ref.shape[4]
    c1 = feats // 2
    mid = n * w1_ref.shape[1]
    out_ch = n * w2_ref.shape[1]
    hplanes, hrows = planes // 2, qs
    hq = hrows // 2
    hpairs = pairs // 2

    has_next_d, has_prev_d = d < n - 1, d > 0
    has_next_r, has_prev_r = r < rows_n - 1, r > 0
    parity = lax.rem(d, 2)
    partner = d + 1 - 2 * parity

    own_x = [
        pltpu.make_async_copy(x_ref.at[:, :, 0], ext.at[1:planes + 1, 0:qs, 1], x_sem.at[0]),
        pltpu.make_async_copy(x_ref.at[:, :, 1], ext.at[1:planes + 1, 1:qs + 1, 0], x_sem.at[1]),
    ]
    for c in own_x:
        c.start()
    own_w2 = pltpu.make_async_copy(w2_ref, g2.at[:, d], own_sem.at[0])
    own_w2.start()

    barrier = pltpu.get_barrier_semaphore()
    relay = n == 8 and rows_n % 2 == 0
    if relay:
        chip, core = d // 2, lax.rem(d, 2)
        x_nbr = chip + 1 - 2 * lax.rem(chip, 2)
        y_nbr = chip + 2 - 4 * (chip // 2)
        mate_r = r + 1 - 2 * lax.rem(r, 2)
        turned = chip == 2
        u_nbr = jnp.where(turned, x_nbr, y_nbr)
        v_nbr = jnp.where(turned, y_nbr, x_nbr)
        g_nbr = 3 - chip
        mine = core == lax.rem(r, 2)
        friends = [(partner, r), (2 * x_nbr + core, r), (2 * y_nbr + core, r), (2 * g_nbr + core, r), (d, mate_r)]
    else:
        friends = [(lax.rem(d + k, n), r) for k in range(1, n)]
    for to in friends:
        pl.semaphore_signal(barrier, inc=1, device_id=to, device_id_type=MESH)

    @pl.when(has_prev_d)
    def _():
        pl.semaphore_signal(barrier, inc=1, device_id=(d - 1, r), device_id_type=MESH)

    @pl.when(has_prev_r)
    def _():
        pl.semaphore_signal(barrier, inc=1, device_id=(d, r - 1), device_id_type=MESH)

    @pl.when(has_prev_r & has_prev_d)
    def _():
        pl.semaphore_signal(barrier, inc=1, device_id=(d - 1, r - 1), device_id_type=MESH)

    zero_half = jnp.zeros((w1_ref.shape[1], c1), BF16)
    for ij in range(9):
        g1[ij, d] = jnp.concatenate([w1_ref[3 * ij + 1], w1_ref[3 * ij + 2]], 1)
        g1[9 + ij, d] = jnp.concatenate([zero_half, w1_ref[3 * ij]], 1)

    @pl.when(jnp.logical_not(has_prev_d))
    def _():
        ext[0] = jnp.zeros(ext.shape[1:], BF16)
        hid[0] = jnp.zeros(hid.shape[1:], BF16)

    @pl.when(jnp.logical_not(has_prev_r))
    def _():
        ext[:, 0, 0] = jnp.zeros((planes + 1, pairs, feats), BF16)
        hid[:, 0, 0] = jnp.zeros((hplanes + 1, hpairs, 2 * mid), BF16)

    expected = (len(friends) + has_next_d.astype(jnp.int32) + has_next_r.astype(jnp.int32)
                + (has_next_r & has_next_d).astype(jnp.int32))
    pl.semaphore_wait(barrier, expected)

    def remote(src, dst, ssem, rsem, to):
        return pltpu.make_async_remote_copy(
            src_ref=src, dst_ref=dst, send_sem=ssem, recv_sem=rsem,
            device_id=to, device_id_type=MESH)

    def when_start(cond, copies):
        @pl.when(cond)
        def _():
            for c in copies:
                c.start()

    def when_recv(cond, copies):
        @pl.when(cond)
        def _():
            for c in copies:
                c.wait_recv()

    def when_sent(cond, copies):
        @pl.when(cond)
        def _():
            for c in copies:
                c.wait_send()

    always = n > 0
    sent = []

    class Gather:
        def __init__(self, buf, own, ssem, rsem, cuts, relay):
            self.buf, self.own, self.ssem, self.rsem = buf, own, ssem, rsem
            self.cuts = list(zip(cuts[:-1], cuts[1:]))
            self.used = 0
            self.relay = relay

        def copy(self, owner, j, to, own=False):
            lo, hi = self.cuts[j]
            place = self.buf.at[lo:hi, owner]
            c = remote(self.own.at[lo:hi] if own else place, place, self.ssem.at[self.used],
                       self.rsem.at[owner * len(self.cuts) + j], to)
            self.used += 1
            return c

        def send(self, cond, owner, j, to, own=False):
            c = self.copy(owner, j, to, own)
            sent.append((cond, c))
            if cond is always:
                c.start()
            else:
                when_start(cond, [c])

        def wait(self, owner, j):
            lo, hi = self.cuts[j]
            place = self.buf.at[lo:hi, owner]
            sem = self.rsem.at[owner * len(self.cuts) + j]
            remote(place, place, sem, sem, (partner, r)).wait_recv()

        def send_own(self):
            for j in range(len(self.cuts)):
                if self.relay:
                    self.send((chip == 3) | mine, d, j, (2 * x_nbr + core, r), True)
                    self.send((chip != 0) | mine, d, j, (2 * y_nbr + core, r), True)
                else:
                    for k in range(1, n // 2):
                        self.send(always, d, j, (lax.rem(d + 2 * k, n), r), True)
            for j in range(len(self.cuts)):
                self.send(always, d, j, (partner, r), True)

        def stage(self, which, j):
            if not self.relay:
                if which == "g":
                    for k in range(1, n // 2):
                        self.wait(lax.rem(d + 2 * k, n), j)
                        self.send(always, lax.rem(d + 2 * k, n), j, (partner, r))
                return
            owner = 2 * {"u": u_nbr, "v": v_nbr, "g": g_nbr}[which] + core
            self.wait(owner, j)
            if which == "u":
                self.send(mine & (chip >= 2), owner, j, (2 * jnp.where(turned, y_nbr, x_nbr) + core, r))
            if which == "v":
                self.send(mine & ((chip == 1) | (chip == 3)), owner, j, (2 * y_nbr + core, r))
            if which != "u":
                self.send(mine, owner, j, (d, mate_r))
            self.send(always, owner, j, (partner, r))

        def rest(self):
            for j in range(len(self.cuts)):
                for k in range(0, n // 2):
                    self.wait(lax.rem(partner + 2 * k, n), j)

    gather1 = Gather(g1, g1.at[:, d], w1_send, w1_recv, CUTS1, False)
    gather2 = Gather(g2, w2_ref, w2_send, w2_recv, CUTS2, relay)

    next_d, next_r = lax.rem(d + 1, n), lax.rem(r + 1, rows_n)
    plane_out = [
        remote(x_ref.at[planes - 1, :, 0], ext.at[0, 0:qs, 1], h_send.at[0], h_recv.at[0], (next_d, r)),
        remote(x_ref.at[planes - 1, :, 1], ext.at[0, 1:qs + 1, 0], h_send.at[1], h_recv.at[1], (next_d, r)),
    ]
    row_out = [remote(x_ref.at[:, qs - 1, 1], ext.at[1:planes + 1, 0, 0], h_send.at[2], h_recv.at[2], (d, next_r))]
    corner_out = [remote(x_ref.at[planes - 1, qs - 1, 1], ext.at[0, 0, 0], h_send.at[3], h_recv.at[3], (next_d, next_r))]

    gather1.send_own()
    when_start(has_next_r, row_out)
    gather2.send_own()
    when_start(has_next_d, plane_out)
    when_start(has_next_d & has_next_r, corner_out)

    for which in "uvg":
        for j in range(len(CUTS1) - 1):
            gather1.stage(which, j)
    gather1.rest()
    for c in own_x:
        c.wait()
    when_recv(has_prev_r, row_out)

    rhs1 = jnp.concatenate(
        [jnp.concatenate([merged(g1[ij]), merged(g1[9 + ij])], 0) for ij in range(9)], 1)

    def first(a):
        wins = []
        for i in range(3):
            for j in range(3):
                w = ext[2 * a + i, j // 2:j // 2 + qs, j % 2]
                wins.append(w.reshape(qs * pairs, feats))
        res = dot_nt(jnp.concatenate(wins, 1), rhs1)
        val = jnp.maximum(res[:, :mid] + shift_pairs(res[:, mid:], pairs), 0.0)
        tmp[...] = val
        half = qs * hpairs
        for s in range(2):
            part = tmp[pl.ds(s, half, 2), :].astype(BF16).reshape(hq, 2, hpairs, mid)
            hid[a + 1, 0:hq, 1, :, s * mid:(s + 1) * mid] = part[:, 0]
            hid[a + 1, 1:hq + 1, 0, :, s * mid:(s + 1) * mid] = part[:, 1]

    last = hplanes
    hplane_out = [
        remote(hid.at[last, 0:hq, 1], hid.at[0, 0:hq, 1], hh_send.at[0], hh_recv.at[0], (next_d, r)),
        remote(hid.at[last, 1:hq + 1, 0], hid.at[0, 1:hq + 1, 0], hh_send.at[1], hh_recv.at[1], (next_d, r)),
    ]
    hcorner_out = [remote(hid.at[last, hq, 0], hid.at[0, 0, 0], hh_send.at[2], hh_recv.at[2], (next_d, next_r))]
    hrow_out = [remote(hid.at[a + 1, hq, 0], hid.at[a + 1, 0, 0], hh_send.at[3 + a], hh_recv.at[3 + a], (d, next_r))
                for a in range(hplanes)]

    for a in range(hplanes - 1, -1, -1):
        if a == 0:
            when_recv(has_prev_d, plane_out)
            when_recv(has_prev_d & has_prev_r, corner_out)
        first(a)
        if a == hplanes - 1:
            when_start(has_next_d, hplane_out)
            when_start(has_next_d & has_next_r, hcorner_out)
        when_start(has_next_r, [hrow_out[a]])
        if a == hplanes - 1:
            for which in "uv":
                for j in range(len(CUTS2) - 1):
                    gather2.stage(which, j)

    for j in range(len(CUTS2) - 1):
        gather2.stage("g", j)
    gather2.rest()
    own_w2.wait()
    when_recv(has_prev_r, hrow_out)
    when_recv(has_prev_d, hplane_out)
    when_recv(has_prev_d & has_prev_r, hcorner_out)

    for a in range(hplanes // 2):
        wins, rights, ups, lows = [], [], [], []
        for i in range(3):
            for j in range(3):
                w = hid[2 * a + i, j // 2:j // 2 + hq, j % 2].reshape(hq * hpairs, 2 * mid)
                wins.append(w)
                rights.append(w[:, mid:])
                t = 3 * (3 * i + j)
                ups += [merged(g2[t + 1]), merged(g2[t + 2])]
                lows.append(merged(g2[t]))
        up = dot_nt(jnp.concatenate(wins, 1), jnp.concatenate(ups, 1))
        low = dot_nt(jnp.concatenate(rights, 1), jnp.concatenate(lows, 1))
        val = jnp.maximum(up + shift_pairs(low, hpairs), 0.0)
        half = hq * hpairs // 2
        for h in range(out_ch // 128):
            tmp2[h] = val[:, h * 128:(h + 1) * 128]
        for s in range(2):
            for h in range(out_ch // 128):
                part = tmp2[h, pl.ds(s, half, 2), :].astype(BF16).reshape(hq, hpairs // 2, 128)
                at = s * out_ch + h * 128
                o_ref[a, :, :, at:at + 128] = part

    for cond, c in sent:
        when_sent(cond, [c])
    when_sent(has_next_r, row_out + hrow_out)
    when_sent(has_next_d, plane_out + hplane_out)
    when_sent(has_next_d & has_next_r, corner_out + hcorner_out)


def solution(mesh):
    n, rows_n = mesh.shape["depth"], mesh.shape["row"]

    def per_device(x, w1, w2):
        planes, rows, pairs, feats = x.shape
        ch1, ch2 = w1.shape[4], w2.shape[4]
        mid, out_ch = n * ch1, n * ch2
        qs = rows // 2
        hplanes, hq, hpairs = planes // 2, rows // 4, pairs // 2
        x5 = x.reshape(planes, qs, 2, pairs, feats)
        w1t = jnp.transpose(w1, (0, 1, 2, 4, 3)).reshape(27, ch1, w1.shape[3])
        w2t = jnp.transpose(w2, (0, 1, 2, 4, 3)).reshape(27, ch2, w2.shape[3])
        dma = pltpu.SemaphoreType.DMA
        sends = max(n, 11)
        return pl.pallas_call(
            functools.partial(kernel, n, rows_n),
            out_shape=jax.ShapeDtypeStruct((planes // 4, rows // 4, pairs // 4, 2 * out_ch), BF16),
            in_specs=[pl.BlockSpec(memory_space=pl.ANY), pl.BlockSpec(memory_space=pltpu.VMEM),
                      pl.BlockSpec(memory_space=pl.ANY)],
            out_specs=pl.BlockSpec(memory_space=pltpu.VMEM),
            scratch_shapes=[
                pltpu.VMEM((planes + 1, qs + 1, 2, pairs, feats), BF16),
                pltpu.VMEM((18, n, ch1, feats), BF16),
                pltpu.VMEM((27, n, ch2, mid), BF16),
                pltpu.VMEM((hplanes + 1, hq + 1, 2, hpairs, 2 * mid), BF16),
                pltpu.VMEM((qs * pairs, mid), F32),
                pltpu.VMEM((out_ch // 128, hq * hpairs, 128), F32),
                dma((2,)), dma((1,)), dma((4,)), dma((4,)),
                dma((sends * (len(CUTS1) - 1),)), dma((n * (len(CUTS1) - 1),)),
                dma((sends * (len(CUTS2) - 1),)), dma((n * (len(CUTS2) - 1),)),
                dma((3 + hplanes,)), dma((3 + hplanes,)),
            ],
            compiler_params=pltpu.CompilerParams(
                collective_id=0, has_side_effects=True, vmem_limit_bytes=60 * 1024 * 1024),
        )(x5, w1t, w2t)

    return jax.shard_map(
        per_device,
        mesh=mesh,
        in_specs=(
            P("depth", "row", None, None),
            P(None, None, None, None, "depth"),
            P(None, None, None, None, "depth"),
        ),
        out_specs=P("depth", "row", None, None),
        check_vma=False,
    )
```

```python
import functools

import jax
import jax.numpy as jnp
from jax import lax
from jax.experimental import pallas as pl
from jax.experimental.pallas import tpu as pltpu
from jax.sharding import PartitionSpec as P

MESH = pl.DeviceIdType.MESH
BF16, F32 = jnp.bfloat16, jnp.float32
CUTS1 = (0, 18)
CUTS2 = (0, 9, 18, 27)


def dot_nt(lhs, rhs):
    return lax.dot_general(lhs, rhs, (((1,), (1,)), ((), ())), preferred_element_type=F32)


def merged(block):
    n, ch, k = block.shape
    if ch % 16 == 0:
        return block.reshape(n * ch, k)
    return jnp.concatenate([block[s].astype(F32) for s in range(n)], 0).astype(BF16)


def shift_pairs(low, pairs):
    rolled = pltpu.roll(low, 1, 0)
    at = lax.broadcasted_iota(jnp.int32, low.shape, 0)
    return jnp.where(lax.rem(at, pairs) == 0, 0.0, rolled)


def kernel(n, rows_n, x_ref, w1_ref, w2_ref, o_ref, ext, g1, g2, hid, tmp, tmp2,
           x_sem, own_sem, h_send, h_recv, w1_send, w1_recv,
           w2_send, w2_recv, hh_send, hh_recv):
    d, r = lax.axis_index("depth"), lax.axis_index("row")
    planes, qs = x_ref.shape[0], x_ref.shape[1]
    pairs, feats = x_ref.shape[3], x_ref.shape[4]
    c1 = feats // 2
    mid = n * w1_ref.shape[1]
    out_ch = n * w2_ref.shape[1]
    hplanes, hrows = planes // 2, qs
    hq = hrows // 2
    hpairs = pairs // 2

    has_next_d, has_prev_d = d < n - 1, d > 0
    has_next_r, has_prev_r = r < rows_n - 1, r > 0
    parity = lax.rem(d, 2)
    partner = d + 1 - 2 * parity

    own_x = [
        pltpu.make_async_copy(x_ref.at[:, :, 0], ext.at[1:planes + 1, 0:qs, 1], x_sem.at[0]),
        pltpu.make_async_copy(x_ref.at[:, :, 1], ext.at[1:planes + 1, 1:qs + 1, 0], x_sem.at[1]),
    ]
    for c in own_x:
        c.start()
    own_w2 = pltpu.make_async_copy(w2_ref, g2.at[:, d], own_sem.at[0])
    own_w2.start()

    barrier = pltpu.get_barrier_semaphore()
    relay = n == 8 and rows_n % 2 == 0
    if relay:
        chip, core = d // 2, lax.rem(d, 2)
        x_nbr = chip + 1 - 2 * lax.rem(chip, 2)
        y_nbr = chip + 2 - 4 * (chip // 2)
        mate_r = r + 1 - 2 * lax.rem(r, 2)
        turned = chip == 2
        u_nbr = jnp.where(turned, x_nbr, y_nbr)
        v_nbr = jnp.where(turned, y_nbr, x_nbr)
        g_nbr = 3 - chip
        mine = core == lax.rem(r, 2)
        friends = [(partner, r), (2 * x_nbr + core, r), (2 * y_nbr + core, r), (2 * g_nbr + core, r), (d, mate_r)]
    else:
        friends = [(lax.rem(d + k, n), r) for k in range(1, n)]
    for to in friends:
        pl.semaphore_signal(barrier, inc=1, device_id=to, device_id_type=MESH)

    @pl.when(has_prev_d)
    def _():
        pl.semaphore_signal(barrier, inc=1, device_id=(d - 1, r), device_id_type=MESH)

    @pl.when(has_prev_r)
    def _():
        pl.semaphore_signal(barrier, inc=1, device_id=(d, r - 1), device_id_type=MESH)

    @pl.when(has_prev_r & has_prev_d)
    def _():
        pl.semaphore_signal(barrier, inc=1, device_id=(d - 1, r - 1), device_id_type=MESH)

    zero_half = jnp.zeros((w1_ref.shape[1], c1), BF16)
    for ij in range(9):
        g1[ij, d] = jnp.concatenate([w1_ref[3 * ij + 1], w1_ref[3 * ij + 2]], 1)
        g1[9 + ij, d] = jnp.concatenate([zero_half, w1_ref[3 * ij]], 1)

    @pl.when(jnp.logical_not(has_prev_d))
    def _():
        ext[0] = jnp.zeros(ext.shape[1:], BF16)
        hid[0] = jnp.zeros(hid.shape[1:], BF16)

    @pl.when(jnp.logical_not(has_prev_r))
    def _():
        ext[:, 0, 0] = jnp.zeros((planes + 1, pairs, feats), BF16)
        hid[:, 0, 0] = jnp.zeros((hplanes + 1, hpairs, 2 * mid), BF16)

    expected = (len(friends) + has_next_d.astype(jnp.int32) + has_next_r.astype(jnp.int32)
                + (has_next_r & has_next_d).astype(jnp.int32))
    pl.semaphore_wait(barrier, expected)

    def remote(src, dst, ssem, rsem, to):
        return pltpu.make_async_remote_copy(
            src_ref=src, dst_ref=dst, send_sem=ssem, recv_sem=rsem,
            device_id=to, device_id_type=MESH)

    def when_start(cond, copies):
        @pl.when(cond)
        def _():
            for c in copies:
                c.start()

    def when_recv(cond, copies):
        @pl.when(cond)
        def _():
            for c in copies:
                c.wait_recv()

    def when_sent(cond, copies):
        @pl.when(cond)
        def _():
            for c in copies:
                c.wait_send()

    always = n > 0
    sent = []

    class Gather:
        def __init__(self, buf, own, ssem, rsem, cuts, relay):
            self.buf, self.own, self.ssem, self.rsem = buf, own, ssem, rsem
            self.cuts = list(zip(cuts[:-1], cuts[1:]))
            self.used = 0
            self.relay = relay

        def copy(self, owner, j, to, own=False):
            lo, hi = self.cuts[j]
            place = self.buf.at[lo:hi, owner]
            c = remote(self.own.at[lo:hi] if own else place, place, self.ssem.at[self.used],
                       self.rsem.at[owner * len(self.cuts) + j], to)
            self.used += 1
            return c

        def send(self, cond, owner, j, to, own=False):
            c = self.copy(owner, j, to, own)
            sent.append((cond, c))
            if cond is always:
                c.start()
            else:
                when_start(cond, [c])

        def wait(self, owner, j):
            lo, hi = self.cuts[j]
            place = self.buf.at[lo:hi, owner]
            sem = self.rsem.at[owner * len(self.cuts) + j]
            remote(place, place, sem, sem, (partner, r)).wait_recv()

        def send_own(self, part):
            for j in range(len(self.cuts)):
                if self.relay and part == "v":
                    self.send(mine & (chip != 3), d, j, (2 * x_nbr + core, r), True)
                    self.send(mine & (chip == 0), d, j, (2 * y_nbr + core, r), True)
                if self.relay and part == "u":
                    self.send(chip != 0, d, j, (2 * y_nbr + core, r), True)
                    self.send(chip == 3, d, j, (2 * x_nbr + core, r), True)
                if not self.relay and part == "u":
                    for k in range(1, n // 2):
                        self.send(always, d, j, (lax.rem(d + 2 * k, n), r), True)
            if part == "u":
                for j in range(len(self.cuts)):
                    self.send(always, d, j, (partner, r), True)

        def stage(self, which, j, direct):
            if not self.relay:
                if which == "g" and direct:
                    for k in range(1, n // 2):
                        self.wait(lax.rem(d + 2 * k, n), j)
                        self.send(always, lax.rem(d + 2 * k, n), j, (partner, r))
                return
            owner = 2 * {"u": u_nbr, "v": v_nbr, "g": g_nbr}[which] + core
            if which == "u":
                self.wait(owner, j)
                self.send(mine & (chip >= 2), owner, j, (2 * jnp.where(turned, y_nbr, x_nbr) + core, r))
                self.send(always, owner, j, (partner, r))
                return
            here = mine if direct else jnp.logical_not(mine)

            @pl.when(here)
            def _():
                self.wait(owner, j)

            if direct:
                if which == "v":
                    self.send(mine & ((chip == 1) | (chip == 3)), owner, j, (2 * y_nbr + core, r))
                self.send(mine, owner, j, (d, mate_r))
            self.send(here, owner, j, (partner, r))

        def rest(self):
            for j in range(len(self.cuts)):
                for k in range(0, n // 2):
                    self.wait(lax.rem(partner + 2 * k, n), j)

    gather1 = Gather(g1, g1.at[:, d], w1_send, w1_recv, CUTS1, False)
    gather2 = Gather(g2, w2_ref, w2_send, w2_recv, CUTS2, relay)

    next_d, next_r = lax.rem(d + 1, n), lax.rem(r + 1, rows_n)
    plane_out = [
        remote(x_ref.at[planes - 1, :, 0], ext.at[0, 0:qs, 1], h_send.at[0], h_recv.at[0], (next_d, r)),
        remote(x_ref.at[planes - 1, :, 1], ext.at[0, 1:qs + 1, 0], h_send.at[1], h_recv.at[1], (next_d, r)),
    ]
    row_out = [remote(x_ref.at[:, qs - 1, 1], ext.at[1:planes + 1, 0, 0], h_send.at[2], h_recv.at[2], (d, next_r))]
    corner_out = [remote(x_ref.at[planes - 1, qs - 1, 1], ext.at[0, 0, 0], h_send.at[3], h_recv.at[3], (next_d, next_r))]

    pieces1, pieces2 = range(len(CUTS1) - 1), range(len(CUTS2) - 1)
    gather1.send_own("u")
    gather2.send_own("v")
    when_start(has_next_r, row_out)
    when_start(has_next_d, plane_out)
    when_start(has_next_d & has_next_r, corner_out)
    gather2.send_own("u")

    for which, direct in (("u", True), ("v", False), ("g", True)):
        pass
    for j in pieces1:
        gather1.stage("g", j, True)
    gather1.rest()
    for j in pieces2:
        gather2.stage("v", j, True)
    for c in own_x:
        c.wait()
    when_recv(has_prev_r, row_out)

    rhs1 = jnp.concatenate(
        [jnp.concatenate([merged(g1[ij]), merged(g1[9 + ij])], 0) for ij in range(9)], 1)

    def first(a):
        wins = []
        for i in range(3):
            for j in range(3):
                w = ext[2 * a + i, j // 2:j // 2 + qs, j % 2]
                wins.append(w.reshape(qs * pairs, feats))
        res = dot_nt(jnp.concatenate(wins, 1), rhs1)
        val = jnp.maximum(res[:, :mid] + shift_pairs(res[:, mid:], pairs), 0.0)
        tmp[...] = val
        half = qs * hpairs
        for s in range(2):
            part = tmp[pl.ds(s, half, 2), :].astype(BF16).reshape(hq, 2, hpairs, mid)
            hid[a + 1, 0:hq, 1, :, s * mid:(s + 1) * mid] = part[:, 0]
            hid[a + 1, 1:hq + 1, 0, :, s * mid:(s + 1) * mid] = part[:, 1]

    last = hplanes
    hplane_out = [
        remote(hid.at[last, 0:hq, 1], hid.at[0, 0:hq, 1], hh_send.at[0], hh_recv.at[0], (next_d, r)),
        remote(hid.at[last, 1:hq + 1, 0], hid.at[0, 1:hq + 1, 0], hh_send.at[1], hh_recv.at[1], (next_d, r)),
    ]
    hcorner_out = [remote(hid.at[last, hq, 0], hid.at[0, 0, 0], hh_send.at[2], hh_recv.at[2], (next_d, next_r))]
    hrow_out = [remote(hid.at[a + 1, hq, 0], hid.at[a + 1, 0, 0], hh_send.at[3 + a], hh_recv.at[3 + a], (d, next_r))
                for a in range(hplanes)]

    for a in range(hplanes - 1, -1, -1):
        if a == 0:
            when_recv(has_prev_d, plane_out)
            when_recv(has_prev_d & has_prev_r, corner_out)
        first(a)
        if a == hplanes - 1:
            when_start(has_next_d, hplane_out)
            when_start(has_next_d & has_next_r, hcorner_out)
        when_start(has_next_r, [hrow_out[a]])
        if a == hplanes - 1:
            for which, direct in (("u", True), ("v", False), ("g", True)):
                for j in pieces2:
                    gather2.stage(which, j, direct)

    for j in pieces2:
        gather2.stage("g", j, False)
    gather2.rest()
    own_w2.wait()
    when_recv(has_prev_r, hrow_out)
    when_recv(has_prev_d, hplane_out)
    when_recv(has_prev_d & has_prev_r, hcorner_out)

    for a in range(hplanes // 2):
        wins, rights, ups, lows = [], [], [], []
        for i in range(3):
            for j in range(3):
                w = hid[2 * a + i, j // 2:j // 2 + hq, j % 2].reshape(hq * hpairs, 2 * mid)
                wins.append(w)
                rights.append(w[:, mid:])
                t = 3 * (3 * i + j)
                ups += [merged(g2[t + 1]), merged(g2[t + 2])]
                lows.append(merged(g2[t]))
        up = dot_nt(jnp.concatenate(wins, 1), jnp.concatenate(ups, 1))
        low = dot_nt(jnp.concatenate(rights, 1), jnp.concatenate(lows, 1))
        val = jnp.maximum(up + shift_pairs(low, hpairs), 0.0)
        half = hq * hpairs // 2
        for h in range(out_ch // 128):
            tmp2[h] = val[:, h * 128:(h + 1) * 128]
        for s in range(2):
            for h in range(out_ch // 128):
                part = tmp2[h, pl.ds(s, half, 2), :].astype(BF16).reshape(hq, hpairs // 2, 128)
                at = s * out_ch + h * 128
                o_ref[a, :, :, at:at + 128] = part

    for cond, c in sent:
        when_sent(cond, [c])
    when_sent(has_next_r, row_out + hrow_out)
    when_sent(has_next_d, plane_out + hplane_out)
    when_sent(has_next_d & has_next_r, corner_out + hcorner_out)


def solution(mesh):
    n, rows_n = mesh.shape["depth"], mesh.shape["row"]

    def per_device(x, w1, w2):
        planes, rows, pairs, feats = x.shape
        ch1, ch2 = w1.shape[4], w2.shape[4]
        mid, out_ch = n * ch1, n * ch2
        qs = rows // 2
        hplanes, hq, hpairs = planes // 2, rows // 4, pairs // 2
        x5 = x.reshape(planes, qs, 2, pairs, feats)
        w1t = jnp.transpose(w1, (0, 1, 2, 4, 3)).reshape(27, ch1, w1.shape[3])
        w2t = jnp.transpose(w2, (0, 1, 2, 4, 3)).reshape(27, ch2, w2.shape[3])
        dma = pltpu.SemaphoreType.DMA
        sends = max(n, 14)
        return pl.pallas_call(
            functools.partial(kernel, n, rows_n),
            out_shape=jax.ShapeDtypeStruct((planes // 4, rows // 4, pairs // 4, 2 * out_ch), BF16),
            in_specs=[pl.BlockSpec(memory_space=pl.ANY), pl.BlockSpec(memory_space=pltpu.VMEM),
                      pl.BlockSpec(memory_space=pl.ANY)],
            out_specs=pl.BlockSpec(memory_space=pltpu.VMEM),
            scratch_shapes=[
                pltpu.VMEM((planes + 1, qs + 1, 2, pairs, feats), BF16),
                pltpu.VMEM((18, n, ch1, feats), BF16),
                pltpu.VMEM((27, n, ch2, mid), BF16),
                pltpu.VMEM((hplanes + 1, hq + 1, 2, hpairs, 2 * mid), BF16),
                pltpu.VMEM((qs * pairs, mid), F32),
                pltpu.VMEM((out_ch // 128, hq * hpairs, 128), F32),
                dma((2,)), dma((1,)), dma((4,)), dma((4,)),
                dma((sends * (len(CUTS1) - 1),)), dma((n * (len(CUTS1) - 1),)),
                dma((sends * (len(CUTS2) - 1),)), dma((n * (len(CUTS2) - 1),)),
                dma((3 + hplanes,)), dma((3 + hplanes,)),
            ],
            compiler_params=pltpu.CompilerParams(
                collective_id=0, has_side_effects=True, vmem_limit_bytes=60 * 1024 * 1024),
        )(x5, w1t, w2t)

    return jax.shard_map(
        per_device,
        mesh=mesh,
        in_specs=(
            P("depth", "row", None, None),
            P(None, None, None, None, "depth"),
            P(None, None, None, None, "depth"),
        ),
        out_specs=P("depth", "row", None, None),
        check_vma=False,
    )
```

```python
import functools

import jax
import jax.numpy as jnp
from jax import lax
from jax.experimental import pallas as pl
from jax.experimental.pallas import tpu as pltpu
from jax.sharding import PartitionSpec as P

MESH = pl.DeviceIdType.MESH
BF16, F32 = jnp.bfloat16, jnp.float32
CUTS1 = (0, 18)
CUTS2 = (0, 9, 18, 27)


def dot_nt(lhs, rhs):
    return lax.dot_general(lhs, rhs, (((1,), (1,)), ((), ())), preferred_element_type=F32)


def merged(block):
    n, ch, k = block.shape
    if ch % 16 == 0:
        return block.reshape(n * ch, k)
    return jnp.concatenate([block[s].astype(F32) for s in range(n)], 0).astype(BF16)


def shift_pairs(low, pairs):
    rolled = pltpu.roll(low, 1, 0)
    at = lax.broadcasted_iota(jnp.int32, low.shape, 0)
    return jnp.where(lax.rem(at, pairs) == 0, 0.0, rolled)


def kernel(n, rows_n, x_ref, w1_ref, w2_ref, o_ref, ext, g1, g2, hid, tmp, tmp2,
           x_sem, own_sem, h_send, h_recv, w1_send, w1_recv,
           w2_send, w2_recv, hh_send, hh_recv):
    d, r = lax.axis_index("depth"), lax.axis_index("row")
    planes, qs = x_ref.shape[0], x_ref.shape[1]
    pairs, feats = x_ref.shape[3], x_ref.shape[4]
    c1 = feats // 2
    mid = n * w1_ref.shape[1]
    out_ch = n * w2_ref.shape[1]
    hplanes, hrows = planes // 2, qs
    hq = hrows // 2
    hpairs = pairs // 2

    has_next_d, has_prev_d = d < n - 1, d > 0
    has_next_r, has_prev_r = r < rows_n - 1, r > 0
    parity = lax.rem(d, 2)
    partner = d + 1 - 2 * parity

    own_x = [
        pltpu.make_async_copy(x_ref.at[:, :, 0], ext.at[1:planes + 1, 0:qs, 1], x_sem.at[0]),
        pltpu.make_async_copy(x_ref.at[:, :, 1], ext.at[1:planes + 1, 1:qs + 1, 0], x_sem.at[1]),
    ]
    for c in own_x:
        c.start()
    own_w2 = pltpu.make_async_copy(w2_ref, g2.at[:, d], own_sem.at[0])
    own_w2.start()

    barrier = pltpu.get_barrier_semaphore()
    relay = n == 8 and rows_n % 2 == 0
    if relay:
        chip, core = d // 2, lax.rem(d, 2)
        x_nbr = chip + 1 - 2 * lax.rem(chip, 2)
        y_nbr = chip + 2 - 4 * (chip // 2)
        mate_r = r + 1 - 2 * lax.rem(r, 2)
        turned = chip == 2
        u_nbr = jnp.where(turned, x_nbr, y_nbr)
        v_nbr = jnp.where(turned, y_nbr, x_nbr)
        g_nbr = 3 - chip
        mine = core == lax.rem(r, 2)
        friends = [(partner, r), (2 * x_nbr + core, r), (2 * y_nbr + core, r), (2 * g_nbr + core, r), (d, mate_r)]
    else:
        friends = [(lax.rem(d + k, n), r) for k in range(1, n)]
    for to in friends:
        pl.semaphore_signal(barrier, inc=1, device_id=to, device_id_type=MESH)

    @pl.when(has_prev_d)
    def _():
        pl.semaphore_signal(barrier, inc=1, device_id=(d - 1, r), device_id_type=MESH)

    @pl.when(has_prev_r)
    def _():
        pl.semaphore_signal(barrier, inc=1, device_id=(d, r - 1), device_id_type=MESH)

    @pl.when(has_prev_r & has_prev_d)
    def _():
        pl.semaphore_signal(barrier, inc=1, device_id=(d - 1, r - 1), device_id_type=MESH)

    zero_half = jnp.zeros((w1_ref.shape[1], c1), BF16)
    for ij in range(9):
        g1[ij, d] = jnp.concatenate([w1_ref[3 * ij + 1], w1_ref[3 * ij + 2]], 1)
        g1[9 + ij, d] = jnp.concatenate([zero_half, w1_ref[3 * ij]], 1)

    @pl.when(jnp.logical_not(has_prev_d))
    def _():
        ext[0] = jnp.zeros(ext.shape[1:], BF16)
        hid[0] = jnp.zeros(hid.shape[1:], BF16)

    @pl.when(jnp.logical_not(has_prev_r))
    def _():
        ext[:, 0, 0] = jnp.zeros((planes + 1, pairs, feats), BF16)
        hid[:, 0, 0] = jnp.zeros((hplanes + 1, hpairs, 2 * mid), BF16)

    expected = (len(friends) + has_next_d.astype(jnp.int32) + has_next_r.astype(jnp.int32)
                + (has_next_r & has_next_d).astype(jnp.int32))
    pl.semaphore_wait(barrier, expected)

    def remote(src, dst, ssem, rsem, to):
        return pltpu.make_async_remote_copy(
            src_ref=src, dst_ref=dst, send_sem=ssem, recv_sem=rsem,
            device_id=to, device_id_type=MESH)

    def when_start(cond, copies):
        @pl.when(cond)
        def _():
            for c in copies:
                c.start()

    def when_recv(cond, copies):
        @pl.when(cond)
        def _():
            for c in copies:
                c.wait_recv()

    def when_sent(cond, copies):
        @pl.when(cond)
        def _():
            for c in copies:
                c.wait_send()

    always = n > 0
    sent = []

    class Gather:
        def __init__(self, buf, own, ssem, rsem, cuts, relay):
            self.buf, self.own, self.ssem, self.rsem = buf, own, ssem, rsem
            self.cuts = list(zip(cuts[:-1], cuts[1:]))
            self.used = 0
            self.relay = relay

        def copy(self, owner, j, to, own=False):
            lo, hi = self.cuts[j]
            place = self.buf.at[lo:hi, owner]
            c = remote(self.own.at[lo:hi] if own else place, place, self.ssem.at[self.used],
                       self.rsem.at[owner * len(self.cuts) + j], to)
            self.used += 1
            return c

        def send(self, cond, owner, j, to, own=False):
            c = self.copy(owner, j, to, own)
            sent.append((cond, c))
            if cond is always:
                c.start()
            else:
                when_start(cond, [c])

        def wait(self, owner, j):
            lo, hi = self.cuts[j]
            place = self.buf.at[lo:hi, owner]
            sem = self.rsem.at[owner * len(self.cuts) + j]
            remote(place, place, sem, sem, (partner, r)).wait_recv()

        def send_own(self, part):
            for j in range(len(self.cuts)):
                if self.relay and part == "v":
                    self.send(mine & (chip != 3), d, j, (2 * x_nbr + core, r), True)
                    self.send(mine & (chip == 0), d, j, (2 * y_nbr + core, r), True)
                if self.relay and part == "u":
                    self.send(chip != 0, d, j, (2 * y_nbr + core, r), True)
                    self.send(chip == 3, d, j, (2 * x_nbr + core, r), True)
                if not self.relay and part == "u":
                    for k in range(1, n // 2):
                        self.send(always, d, j, (lax.rem(d + 2 * k, n), r), True)
            if part == "u":
                for j in range(len(self.cuts)):
                    self.send(always, d, j, (partner, r), True)

        def stage(self, which, j, direct):
            if not self.relay:
                if which == "g" and direct:
                    for k in range(1, n // 2):
                        self.wait(lax.rem(d + 2 * k, n), j)
                        self.send(always, lax.rem(d + 2 * k, n), j, (partner, r))
                return
            owner = 2 * {"u": u_nbr, "v": v_nbr, "g": g_nbr}[which] + core
            if which == "u":
                self.wait(owner, j)
                self.send(mine & (chip >= 2), owner, j, (2 * jnp.where(turned, y_nbr, x_nbr) + core, r))
                self.send(always, owner, j, (partner, r))
                return
            here = mine if direct else jnp.logical_not(mine)

            @pl.when(here)
            def _():
                self.wait(owner, j)

            if direct:
                if which == "v":
                    self.send(mine & ((chip == 1) | (chip == 3)), owner, j, (2 * y_nbr + core, r))
                self.send(mine, owner, j, (d, mate_r))
            self.send(here, owner, j, (partner, r))

        def rest(self):
            for j in range(len(self.cuts)):
                for k in range(0, n // 2):
                    self.wait(lax.rem(partner + 2 * k, n), j)

    gather1 = Gather(g1, g1.at[:, d], w1_send, w1_recv, CUTS1, False)
    gather2 = Gather(g2, w2_ref, w2_send, w2_recv, CUTS2, relay)

    next_d, next_r = lax.rem(d + 1, n), lax.rem(r + 1, rows_n)
    plane_out = [
        remote(x_ref.at[planes - 1, :, 0], ext.at[0, 0:qs, 1], h_send.at[0], h_recv.at[0], (next_d, r)),
        remote(x_ref.at[planes - 1, :, 1], ext.at[0, 1:qs + 1, 0], h_send.at[1], h_recv.at[1], (next_d, r)),
    ]
    row_out = [remote(x_ref.at[:, qs - 1, 1], ext.at[1:planes + 1, 0, 0], h_send.at[2], h_recv.at[2], (d, next_r))]
    corner_out = [remote(x_ref.at[planes - 1, qs - 1, 1], ext.at[0, 0, 0], h_send.at[3], h_recv.at[3], (next_d, next_r))]

    pieces1, pieces2 = range(len(CUTS1) - 1), range(len(CUTS2) - 1)
    gather1.send_own("u")
    gather2.send_own("v")
    when_start(has_next_r, row_out)
    gather2.send_own("u")

    for which, direct in (("u", True), ("v", False), ("g", True)):
        pass
    for j in pieces1:
        gather1.stage("g", j, True)
    when_start(has_next_d, plane_out)
    when_start(has_next_d & has_next_r, corner_out)
    gather1.rest()
    for j in pieces2:
        gather2.stage("v", j, True)
    for c in own_x:
        c.wait()
    when_recv(has_prev_r, row_out)

    rhs1 = jnp.concatenate(
        [jnp.concatenate([merged(g1[ij]), merged(g1[9 + ij])], 0) for ij in range(9)], 1)

    def first(a):
        wins = []
        for i in range(3):
            for j in range(3):
                w = ext[2 * a + i, j // 2:j // 2 + qs, j % 2]
                wins.append(w.reshape(qs * pairs, feats))
        res = dot_nt(jnp.concatenate(wins, 1), rhs1)
        val = jnp.maximum(res[:, :mid] + shift_pairs(res[:, mid:], pairs), 0.0)
        tmp[...] = val
        half = qs * hpairs
        for s in range(2):
            part = tmp[pl.ds(s, half, 2), :].astype(BF16).reshape(hq, 2, hpairs, mid)
            hid[a + 1, 0:hq, 1, :, s * mid:(s + 1) * mid] = part[:, 0]
            hid[a + 1, 1:hq + 1, 0, :, s * mid:(s + 1) * mid] = part[:, 1]

    last = hplanes
    hplane_out = [
        remote(hid.at[last, 0:hq, 1], hid.at[0, 0:hq, 1], hh_send.at[0], hh_recv.at[0], (next_d, r)),
        remote(hid.at[last, 1:hq + 1, 0], hid.at[0, 1:hq + 1, 0], hh_send.at[1], hh_recv.at[1], (next_d, r)),
    ]
    hcorner_out = [remote(hid.at[last, hq, 0], hid.at[0, 0, 0], hh_send.at[2], hh_recv.at[2], (next_d, next_r))]
    hrow_out = [remote(hid.at[a + 1, hq, 0], hid.at[a + 1, 0, 0], hh_send.at[3 + a], hh_recv.at[3 + a], (d, next_r))
                for a in range(hplanes)]

    for a in range(hplanes - 1, -1, -1):
        if a == 0:
            when_recv(has_prev_d, plane_out)
            when_recv(has_prev_d & has_prev_r, corner_out)
        first(a)
        if a == hplanes - 1:
            when_start(has_next_d, hplane_out)
            when_start(has_next_d & has_next_r, hcorner_out)
        when_start(has_next_r, [hrow_out[a]])
        if a == hplanes - 1:
            for which, direct in (("u", True), ("v", False), ("g", True)):
                for j in pieces2:
                    gather2.stage(which, j, direct)

    for j in pieces2:
        gather2.stage("g", j, False)
    gather2.rest()
    own_w2.wait()
    when_recv(has_prev_r, hrow_out)
    when_recv(has_prev_d, hplane_out)
    when_recv(has_prev_d & has_prev_r, hcorner_out)

    for a in range(hplanes // 2):
        wins, rights, ups, lows = [], [], [], []
        for i in range(3):
            for j in range(3):
                w = hid[2 * a + i, j // 2:j // 2 + hq, j % 2].reshape(hq * hpairs, 2 * mid)
                wins.append(w)
                rights.append(w[:, mid:])
                t = 3 * (3 * i + j)
                ups += [merged(g2[t + 1]), merged(g2[t + 2])]
                lows.append(merged(g2[t]))
        up = dot_nt(jnp.concatenate(wins, 1), jnp.concatenate(ups, 1))
        low = dot_nt(jnp.concatenate(rights, 1), jnp.concatenate(lows, 1))
        val = jnp.maximum(up + shift_pairs(low, hpairs), 0.0)
        half = hq * hpairs // 2
        for h in range(out_ch // 128):
            tmp2[h] = val[:, h * 128:(h + 1) * 128]
        for s in range(2):
            for h in range(out_ch // 128):
                part = tmp2[h, pl.ds(s, half, 2), :].astype(BF16).reshape(hq, hpairs // 2, 128)
                at = s * out_ch + h * 128
                o_ref[a, :, :, at:at + 128] = part

    for cond, c in sent:
        when_sent(cond, [c])
    when_sent(has_next_r, row_out + hrow_out)
    when_sent(has_next_d, plane_out + hplane_out)
    when_sent(has_next_d & has_next_r, corner_out + hcorner_out)


def solution(mesh):
    n, rows_n = mesh.shape["depth"], mesh.shape["row"]

    def per_device(x, w1, w2):
        planes, rows, pairs, feats = x.shape
        ch1, ch2 = w1.shape[4], w2.shape[4]
        mid, out_ch = n * ch1, n * ch2
        qs = rows // 2
        hplanes, hq, hpairs = planes // 2, rows // 4, pairs // 2
        x5 = x.reshape(planes, qs, 2, pairs, feats)
        w1t = jnp.transpose(w1, (0, 1, 2, 4, 3)).reshape(27, ch1, w1.shape[3])
        w2t = jnp.transpose(w2, (0, 1, 2, 4, 3)).reshape(27, ch2, w2.shape[3])
        dma = pltpu.SemaphoreType.DMA
        sends = max(n, 14)
        return pl.pallas_call(
            functools.partial(kernel, n, rows_n),
            out_shape=jax.ShapeDtypeStruct((planes // 4, rows // 4, pairs // 4, 2 * out_ch), BF16),
            in_specs=[pl.BlockSpec(memory_space=pl.ANY), pl.BlockSpec(memory_space=pltpu.VMEM),
                      pl.BlockSpec(memory_space=pl.ANY)],
            out_specs=pl.BlockSpec(memory_space=pltpu.VMEM),
            scratch_shapes=[
                pltpu.VMEM((planes + 1, qs + 1, 2, pairs, feats), BF16),
                pltpu.VMEM((18, n, ch1, feats), BF16),
                pltpu.VMEM((27, n, ch2, mid), BF16),
                pltpu.VMEM((hplanes + 1, hq + 1, 2, hpairs, 2 * mid), BF16),
                pltpu.VMEM((qs * pairs, mid), F32),
                pltpu.VMEM((out_ch // 128, hq * hpairs, 128), F32),
                dma((2,)), dma((1,)), dma((4,)), dma((4,)),
                dma((sends * (len(CUTS1) - 1),)), dma((n * (len(CUTS1) - 1),)),
                dma((sends * (len(CUTS2) - 1),)), dma((n * (len(CUTS2) - 1),)),
                dma((3 + hplanes,)), dma((3 + hplanes,)),
            ],
            compiler_params=pltpu.CompilerParams(
                collective_id=0, has_side_effects=True, vmem_limit_bytes=60 * 1024 * 1024),
        )(x5, w1t, w2t)

    return jax.shard_map(
        per_device,
        mesh=mesh,
        in_specs=(
            P("depth", "row", None, None),
            P(None, None, None, None, "depth"),
            P(None, None, None, None, "depth"),
        ),
        out_specs=P("depth", "row", None, None),
        check_vma=False,
    )
```

```python
import functools

import jax
import jax.numpy as jnp
from jax import lax
from jax.experimental import pallas as pl
from jax.experimental.pallas import tpu as pltpu
from jax.sharding import PartitionSpec as P

MESH = pl.DeviceIdType.MESH
BF16, F32 = jnp.bfloat16, jnp.float32
CUTS1 = (0, 14)
CUTS2 = (0, 9, 18, 27)


def dot_nt(lhs, rhs):
    return lax.dot_general(lhs, rhs, (((1,), (1,)), ((), ())), preferred_element_type=F32)


def merged(block):
    n, ch, k = block.shape
    if ch % 16 == 0:
        return block.reshape(n * ch, k)
    return jnp.concatenate([block[s].astype(F32) for s in range(n)], 0).astype(BF16)


def shift_pairs(low, pairs):
    rolled = pltpu.roll(low, 1, 0)
    at = lax.broadcasted_iota(jnp.int32, low.shape, 0)
    return jnp.where(lax.rem(at, pairs) == 0, 0.0, rolled)


def kernel(n, rows_n, x_ref, w1_ref, w2_ref, o_ref, ext, g1, g2, hid, tmp, tmp2,
           x_sem, own_sem, h_send, h_recv, w1_send, w1_recv,
           w2_send, w2_recv, hh_send, hh_recv):
    d, r = lax.axis_index("depth"), lax.axis_index("row")
    planes, qs = x_ref.shape[0], x_ref.shape[1]
    pairs, feats = x_ref.shape[3], x_ref.shape[4]
    c1 = feats // 2
    mid = n * w1_ref.shape[1]
    out_ch = n * w2_ref.shape[1]
    hplanes, hrows = planes // 2, qs
    hq = hrows // 2
    hpairs = pairs // 2

    has_next_d, has_prev_d = d < n - 1, d > 0
    has_next_r, has_prev_r = r < rows_n - 1, r > 0
    parity = lax.rem(d, 2)
    partner = d + 1 - 2 * parity

    own_x = [
        pltpu.make_async_copy(x_ref.at[:, :, 0], ext.at[1:planes + 1, 0:qs, 1], x_sem.at[0]),
        pltpu.make_async_copy(x_ref.at[:, :, 1], ext.at[1:planes + 1, 1:qs + 1, 0], x_sem.at[1]),
    ]
    for c in own_x:
        c.start()
    own_w2 = pltpu.make_async_copy(w2_ref, g2.at[:, d], own_sem.at[0])
    own_w2.start()

    barrier = pltpu.get_barrier_semaphore()
    relay = n == 8 and rows_n % 2 == 0
    if relay:
        chip, core = d // 2, lax.rem(d, 2)
        x_nbr = chip + 1 - 2 * lax.rem(chip, 2)
        y_nbr = chip + 2 - 4 * (chip // 2)
        mate_r = r + 1 - 2 * lax.rem(r, 2)
        turned = chip == 2
        u_nbr = jnp.where(turned, x_nbr, y_nbr)
        v_nbr = jnp.where(turned, y_nbr, x_nbr)
        g_nbr = 3 - chip
        mine = core == lax.rem(r, 2)
        friends = [(partner, r), (2 * x_nbr + core, r), (2 * y_nbr + core, r), (2 * g_nbr + core, r), (d, mate_r)]
    else:
        friends = [(lax.rem(d + k, n), r) for k in range(1, n)]
    for to in friends:
        pl.semaphore_signal(barrier, inc=1, device_id=to, device_id_type=MESH)

    @pl.when(has_prev_d)
    def _():
        pl.semaphore_signal(barrier, inc=1, device_id=(d - 1, r), device_id_type=MESH)

    @pl.when(has_prev_r)
    def _():
        pl.semaphore_signal(barrier, inc=1, device_id=(d, r - 1), device_id_type=MESH)

    @pl.when(has_prev_r & has_prev_d)
    def _():
        pl.semaphore_signal(barrier, inc=1, device_id=(d - 1, r - 1), device_id_type=MESH)

    zero_half = jnp.zeros((w1_ref.shape[1], c1), BF16)
    for ij in range(9):
        g1[ij, d] = jnp.concatenate([w1_ref[3 * ij + 1], w1_ref[3 * ij + 2]], 1)
    for m in range(5):
        low = w1_ref[6 * m + 3] if m < 4 else zero_half
        g1[9 + m, d] = jnp.concatenate([low, w1_ref[6 * m]], 1)

    @pl.when(jnp.logical_not(has_prev_d))
    def _():
        ext[0] = jnp.zeros(ext.shape[1:], BF16)
        hid[0] = jnp.zeros(hid.shape[1:], BF16)

    @pl.when(jnp.logical_not(has_prev_r))
    def _():
        ext[:, 0, 0] = jnp.zeros((planes + 1, pairs, feats), BF16)
        hid[:, 0, 0] = jnp.zeros((hplanes + 1, hpairs, 2 * mid), BF16)

    expected = (len(friends) + has_next_d.astype(jnp.int32) + has_next_r.astype(jnp.int32)
                + (has_next_r & has_next_d).astype(jnp.int32))
    pl.semaphore_wait(barrier, expected)

    def remote(src, dst, ssem, rsem, to):
        return pltpu.make_async_remote_copy(
            src_ref=src, dst_ref=dst, send_sem=ssem, recv_sem=rsem,
            device_id=to, device_id_type=MESH)

    def when_start(cond, copies):
        @pl.when(cond)
        def _():
            for c in copies:
                c.start()

    def when_recv(cond, copies):
        @pl.when(cond)
        def _():
            for c in copies:
                c.wait_recv()

    def when_sent(cond, copies):
        @pl.when(cond)
        def _():
            for c in copies:
                c.wait_send()

    always = n > 0
    sent = []

    class Gather:
        def __init__(self, buf, own, ssem, rsem, cuts, relay):
            self.buf, self.own, self.ssem, self.rsem = buf, own, ssem, rsem
            self.cuts = list(zip(cuts[:-1], cuts[1:]))
            self.used = 0
            self.relay = relay

        def copy(self, owner, j, to, own=False):
            lo, hi = self.cuts[j]
            place = self.buf.at[lo:hi, owner]
            c = remote(self.own.at[lo:hi] if own else place, place, self.ssem.at[self.used],
                       self.rsem.at[owner * len(self.cuts) + j], to)
            self.used += 1
            return c

        def send(self, cond, owner, j, to, own=False):
            c = self.copy(owner, j, to, own)
            sent.append((cond, c))
            if cond is always:
                c.start()
            else:
                when_start(cond, [c])

        def wait(self, owner, j):
            lo, hi = self.cuts[j]
            place = self.buf.at[lo:hi, owner]
            sem = self.rsem.at[owner * len(self.cuts) + j]
            remote(place, place, sem, sem, (partner, r)).wait_recv()

        def send_own(self, part):
            for j in range(len(self.cuts)):
                if self.relay and part == "v":
                    self.send(mine & (chip != 3), d, j, (2 * x_nbr + core, r), True)
                    self.send(mine & (chip == 0), d, j, (2 * y_nbr + core, r), True)
                if self.relay and part == "u":
                    self.send(chip != 0, d, j, (2 * y_nbr + core, r), True)
                    self.send(chip == 3, d, j, (2 * x_nbr + core, r), True)
                if not self.relay and part == "u":
                    for k in range(1, n // 2):
                        self.send(always, d, j, (lax.rem(d + 2 * k, n), r), True)
            if part == "u":
                for j in range(len(self.cuts)):
                    self.send(always, d, j, (partner, r), True)

        def stage(self, which, j, direct):
            if not self.relay:
                if which == "g" and direct:
                    for k in range(1, n // 2):
                        self.wait(lax.rem(d + 2 * k, n), j)
                        self.send(always, lax.rem(d + 2 * k, n), j, (partner, r))
                return
            owner = 2 * {"u": u_nbr, "v": v_nbr, "g": g_nbr}[which] + core
            if which == "u":
                self.wait(owner, j)
                self.send(mine & (chip >= 2), owner, j, (2 * jnp.where(turned, y_nbr, x_nbr) + core, r))
                self.send(always, owner, j, (partner, r))
                return
            here = mine if direct else jnp.logical_not(mine)

            @pl.when(here)
            def _():
                self.wait(owner, j)

            if direct:
                if which == "v":
                    self.send(mine & ((chip == 1) | (chip == 3)), owner, j, (2 * y_nbr + core, r))
                self.send(mine, owner, j, (d, mate_r))
            self.send(here, owner, j, (partner, r))

        def rest(self):
            for j in range(len(self.cuts)):
                for k in range(0, n // 2):
                    self.wait(lax.rem(partner + 2 * k, n), j)

    gather1 = Gather(g1, g1.at[:, d], w1_send, w1_recv, CUTS1, False)
    gather2 = Gather(g2, w2_ref, w2_send, w2_recv, CUTS2, relay)

    next_d, next_r = lax.rem(d + 1, n), lax.rem(r + 1, rows_n)
    plane_out = [
        remote(x_ref.at[planes - 1, :, 0], ext.at[0, 0:qs, 1], h_send.at[0], h_recv.at[0], (next_d, r)),
        remote(x_ref.at[planes - 1, :, 1], ext.at[0, 1:qs + 1, 0], h_send.at[1], h_recv.at[1], (next_d, r)),
    ]
    row_out = [remote(x_ref.at[:, qs - 1, 1], ext.at[1:planes + 1, 0, 0], h_send.at[2], h_recv.at[2], (d, next_r))]
    corner_out = [remote(x_ref.at[planes - 1, qs - 1, 1], ext.at[0, 0, 0], h_send.at[3], h_recv.at[3], (next_d, next_r))]

    pieces1, pieces2 = range(len(CUTS1) - 1), range(len(CUTS2) - 1)
    gather1.send_own("u")
    gather2.send_own("v")
    when_start(has_next_r, row_out)
    gather2.send_own("u")

    for which, direct in (("u", True), ("v", False), ("g", True)):
        pass
    for j in pieces1:
        gather1.stage("g", j, True)
    when_start(has_next_d, plane_out)
    when_start(has_next_d & has_next_r, corner_out)
    gather1.rest()
    for j in pieces2:
        gather2.stage("v", j, True)
    for c in own_x:
        c.wait()
    when_recv(has_prev_r, row_out)

    def third(ij):
        tile = merged(g1[9 + ij // 2])
        part = tile[:, c1:] if ij % 2 == 0 else tile[:, :c1]
        return jnp.concatenate([jnp.zeros_like(part), part], 1)

    rhs1 = jnp.concatenate(
        [jnp.concatenate([merged(g1[ij]), third(ij)], 0) for ij in range(9)], 1)

    def first(a):
        wins = []
        for i in range(3):
            for j in range(3):
                w = ext[2 * a + i, j // 2:j // 2 + qs, j % 2]
                wins.append(w.reshape(qs * pairs, feats))
        res = dot_nt(jnp.concatenate(wins, 1), rhs1)
        val = jnp.maximum(res[:, :mid] + shift_pairs(res[:, mid:], pairs), 0.0)
        tmp[...] = val
        half = qs * hpairs
        for s in range(2):
            part = tmp[pl.ds(s, half, 2), :].astype(BF16).reshape(hq, 2, hpairs, mid)
            hid[a + 1, 0:hq, 1, :, s * mid:(s + 1) * mid] = part[:, 0]
            hid[a + 1, 1:hq + 1, 0, :, s * mid:(s + 1) * mid] = part[:, 1]

    last = hplanes
    hplane_out = [
        remote(hid.at[last, 0:hq, 1], hid.at[0, 0:hq, 1], hh_send.at[0], hh_recv.at[0], (next_d, r)),
        remote(hid.at[last, 1:hq + 1, 0], hid.at[0, 1:hq + 1, 0], hh_send.at[1], hh_recv.at[1], (next_d, r)),
    ]
    hcorner_out = [remote(hid.at[last, hq, 0], hid.at[0, 0, 0], hh_send.at[2], hh_recv.at[2], (next_d, next_r))]
    hrow_out = [remote(hid.at[a + 1, hq, 0], hid.at[a + 1, 0, 0], hh_send.at[3 + a], hh_recv.at[3 + a], (d, next_r))
                for a in range(hplanes)]

    for a in range(hplanes - 1, -1, -1):
        if a == 0:
            when_recv(has_prev_d, plane_out)
            when_recv(has_prev_d & has_prev_r, corner_out)
        first(a)
        if a == hplanes - 1:
            when_start(has_next_d, hplane_out)
            when_start(has_next_d & has_next_r, hcorner_out)
        when_start(has_next_r, [hrow_out[a]])
        if a == hplanes - 1:
            for which, direct in (("u", True), ("v", False), ("g", True)):
                for j in pieces2:
                    gather2.stage(which, j, direct)

    for j in pieces2:
        gather2.stage("g", j, False)
    gather2.rest()
    own_w2.wait()
    when_recv(has_prev_r, hrow_out)
    when_recv(has_prev_d, hplane_out)
    when_recv(has_prev_d & has_prev_r, hcorner_out)

    for a in range(hplanes // 2):
        wins, rights, ups, lows = [], [], [], []
        for i in range(3):
            for j in range(3):
                w = hid[2 * a + i, j // 2:j // 2 + hq, j % 2].reshape(hq * hpairs, 2 * mid)
                wins.append(w)
                rights.append(w[:, mid:])
                t = 3 * (3 * i + j)
                ups += [merged(g2[t + 1]), merged(g2[t + 2])]
                lows.append(merged(g2[t]))
        up = dot_nt(jnp.concatenate(wins, 1), jnp.concatenate(ups, 1))
        low = dot_nt(jnp.concatenate(rights, 1), jnp.concatenate(lows, 1))
        val = jnp.maximum(up + shift_pairs(low, hpairs), 0.0)
        half = hq * hpairs // 2
        for h in range(out_ch // 128):
            tmp2[h] = val[:, h * 128:(h + 1) * 128]
        for s in range(2):
            for h in range(out_ch // 128):
                part = tmp2[h, pl.ds(s, half, 2), :].astype(BF16).reshape(hq, hpairs // 2, 128)
                at = s * out_ch + h * 128
                o_ref[a, :, :, at:at + 128] = part

    for cond, c in sent:
        when_sent(cond, [c])
    when_sent(has_next_r, row_out + hrow_out)
    when_sent(has_next_d, plane_out + hplane_out)
    when_sent(has_next_d & has_next_r, corner_out + hcorner_out)


def solution(mesh):
    n, rows_n = mesh.shape["depth"], mesh.shape["row"]

    def per_device(x, w1, w2):
        planes, rows, pairs, feats = x.shape
        ch1, ch2 = w1.shape[4], w2.shape[4]
        mid, out_ch = n * ch1, n * ch2
        qs = rows // 2
        hplanes, hq, hpairs = planes // 2, rows // 4, pairs // 2
        x5 = x.reshape(planes, qs, 2, pairs, feats)
        w1t = jnp.transpose(w1, (0, 1, 2, 4, 3)).reshape(27, ch1, w1.shape[3])
        w2t = jnp.transpose(w2, (0, 1, 2, 4, 3)).reshape(27, ch2, w2.shape[3])
        dma = pltpu.SemaphoreType.DMA
        sends = max(n, 14)
        return pl.pallas_call(
            functools.partial(kernel, n, rows_n),
            out_shape=jax.ShapeDtypeStruct((planes // 4, rows // 4, pairs // 4, 2 * out_ch), BF16),
            in_specs=[pl.BlockSpec(memory_space=pl.ANY), pl.BlockSpec(memory_space=pltpu.VMEM),
                      pl.BlockSpec(memory_space=pl.ANY)],
            out_specs=pl.BlockSpec(memory_space=pltpu.VMEM),
            scratch_shapes=[
                pltpu.VMEM((planes + 1, qs + 1, 2, pairs, feats), BF16),
                pltpu.VMEM((14, n, ch1, feats), BF16),
                pltpu.VMEM((27, n, ch2, mid), BF16),
                pltpu.VMEM((hplanes + 1, hq + 1, 2, hpairs, 2 * mid), BF16),
                pltpu.VMEM((qs * pairs, mid), F32),
                pltpu.VMEM((out_ch // 128, hq * hpairs, 128), F32),
                dma((2,)), dma((1,)), dma((4,)), dma((4,)),
                dma((sends * (len(CUTS1) - 1),)), dma((n * (len(CUTS1) - 1),)),
                dma((sends * (len(CUTS2) - 1),)), dma((n * (len(CUTS2) - 1),)),
                dma((3 + hplanes,)), dma((3 + hplanes,)),
            ],
            compiler_params=pltpu.CompilerParams(
                collective_id=0, has_side_effects=True, vmem_limit_bytes=60 * 1024 * 1024),
        )(x5, w1t, w2t)

    return jax.shard_map(
        per_device,
        mesh=mesh,
        in_specs=(
            P("depth", "row", None, None),
            P(None, None, None, None, "depth"),
            P(None, None, None, None, "depth"),
        ),
        out_specs=P("depth", "row", None, None),
        check_vma=False,
    )
```
